32 devices in a mesh: seq: 8 (over z, y), dp: 4 (over x, core).
Axes of the slice: x: 2, y: 2, z: 4, core: 2. Of those that a mesh axis runs over, the one named last changes fastest.
Arguments:
- out_grad: bfloat16 [4, 1536, 4096], P('dp', 'seq'), may hold values from -6 to 6
- w_out: bfloat16 [2048, 4096], P('dp'), may hold values from -0.125 to 0.125
- queries: bfloat16 [4, 1536, 2048], P('dp', 'seq'), may hold values from -6 to 6
- keys: bfloat16 [4, 1536, 2048], P('dp', 'seq'), may hold values from -6 to 6
- values: bfloat16 [4, 1536, 2048], P('dp', 'seq'), may hold values from -6 to 6
- keep_bits: int32 [4, 1536, 128], P('dp', 'seq'), may hold values from 0 to 65535
- query_later: float32 [4, 16, 128, 128], P('dp'), may hold values from -1.8 to 1.8
Outputs:
- query_grad: bfloat16 [4, 1536, 2048], P('dp', 'seq')
- key_grad: bfloat16 [4, 1536, 2048], P('dp', 'seq')
- value_grad: bfloat16 [4, 1536, 2048], P('dp', 'seq')
The draws below stay inside these ranges and needn't reach their ends.
All inputs are finite; a program needn't handle non-finite values.
Results may differ from the reference program's by a relative error of at most 0.0058.
Values may be sent and summed in bfloat16 or wider, within the bound.
A program may use at most 192 MiB of HBM per device.

```python
import jax
import jax.numpy as jnp
from jax import lax

D = 4096
HEADS = 16
HD = 128
TOK_DEV = 192
INNER = 2048
BATCH = 4
LENGTH = 1536
N_SEQ = 8


def touch_ends(values, rng, least, largest):
    dims = values.shape
    spot = [jax.random.randint(jax.random.fold_in(rng, axis), (), 0, dims[axis]) for axis in range(len(dims))]
    values = values.at[tuple(spot)].set(least)
    longest = dims.index(max(dims))
    spot[longest] = (spot[longest] + 1) % dims[longest]
    return values.at[tuple(spot)].set(largest)


def block_scale(rng, extent, split, least, top_value):
    loudness = 1.0
    for dim, parts in split:
        draws = jax.random.uniform(jax.random.fold_in(jax.random.fold_in(rng, 6), dim), (parts,), jnp.float32, least / len(split), top_value / len(split))
        loudness = loudness * jnp.repeat(jnp.exp(draws), extent[dim] // parts).reshape((-1,) + (1,) * (len(extent) - 1 - dim))
    return loudness


def gaussian(stream_key, shape, spread, most, split=(), kind=jnp.bfloat16):
    values = jax.random.normal(stream_key, shape, jnp.float32) * spread
    if len(split) > 0:
        values = block_scale(stream_key, shape, split, -0.22, 0.18) * values
    return jnp.clip(values, min=-most, max=most).astype(kind)


def setup_inputs(seed: int = 0) -> dict:
    arg_keys = jax.random.split(jax.random.key(seed), 8)
    return {
        "out_grad": gaussian(arg_keys[0], (BATCH, LENGTH, D), 1.0, 6.0, ((0, 4), (1, 8))),
        "w_out": gaussian(arg_keys[1], (INNER, D), INNER ** -0.5, 0.125, ((0, 4),)),
        "queries": gaussian(arg_keys[2], (BATCH, LENGTH, INNER), 1.0, 6.0, ((0, 4), (1, 8))),
        "keys": gaussian(arg_keys[3], (BATCH, LENGTH, INNER), 1.0, 6.0, ((0, 4), (1, 8))),
        "values": gaussian(arg_keys[4], (BATCH, LENGTH, INNER), 1.0, 6.0, ((0, 4), (1, 8))),
        "keep_bits": touch_ends(jax.random.randint(arg_keys[5], (BATCH, LENGTH, INNER // 16), 0, 65536), jax.random.fold_in(arg_keys[5], 1), 0, 65535).astype(jnp.int32),
        "query_later": gaussian(arg_keys[6], (BATCH, HEADS, HD, HD), 0.3, 1.8, ((0, 4),), jnp.float32),
    }


def unpack_flags(word_bits, count):
    bit_shift = jnp.arange(16, dtype=jnp.int32)
    flags = word_bits[..., None] >> bit_shift & 1
    return flags.reshape(word_bits.shape[:-1] + (count,)).astype(jnp.float32)

def round_half(tensor):
    return lax.optimization_barrier(tensor.astype(jnp.bfloat16)).astype(jnp.float32)

def reference(out_grad, w_out, queries, keys, values, keep_bits, query_later):

    def one_sequence(items):
        grad_seq, query_seq, key_seq, value_seq, bits_seq, later_seq = items
        length = grad_seq.shape[0]
        projected = jnp.dot(grad_seq, w_out.T, preferred_element_type=jnp.float32)
        keep_mask = unpack_flags(bits_seq, HEADS * HD)
        position = jnp.arange(length).astype(jnp.float32)
        row_scale = 2.0 / jnp.sqrt(HD * (position + 1.0))
        gated = (projected * keep_mask * row_scale[:, None]).astype(jnp.bfloat16)

        def split_heads(tensor):
            return tensor.reshape(N_SEQ, TOK_DEV, HEADS, HD).astype(jnp.float32)
        query_f = split_heads(query_seq)
        key_f = split_heads(key_seq)
        value_f = split_heads(value_seq)
        gated_f = split_heads(gated)
        key_state = jnp.einsum('nthi,nthj->nhij', key_f, value_f)
        query_state = jnp.einsum('nthi,nthj->nhij', query_f, gated_f)
        zero_state = jnp.zeros_like(key_state[:1])
        key_before = jnp.concatenate([zero_state, jnp.cumsum(key_state, axis=0)[:-1]], axis=0)
        query_after = jnp.concatenate([jnp.cumsum(query_state[::-1], axis=0)[::-1][1:], zero_state], axis=0)
        query_after = query_after + later_seq[None].astype(jnp.float32)
        key_before_b = round_half(key_before)
        query_after_b = round_half(query_after)
        causal_mask = (jnp.arange(TOK_DEV)[:, None] >= jnp.arange(TOK_DEV)[None, :]).astype(jnp.float32)
        grad_scores = round_half(jnp.einsum('nthj,nshj->nhts', gated_f, value_f) * causal_mask)
        attn_scores = round_half(jnp.einsum('nthj,nshj->nhts', query_f, key_f) * causal_mask)
        query_grad = jnp.einsum('nhts,nshi->nthi', grad_scores, key_f) + jnp.einsum('nthj,nhij->nthi', gated_f, key_before_b)
        key_grad = jnp.einsum('nhts,nthi->nshi', grad_scores, query_f) + jnp.einsum('nshj,nhij->nshi', value_f, query_after_b)
        value_grad = jnp.einsum('nhts,nthj->nshj', attn_scores, gated_f) + jnp.einsum('nshi,nhij->nshj', key_f, query_after_b)

        def merge_heads(tensor):
            return tensor.reshape(length, HEADS * HD).astype(jnp.bfloat16)
        return (merge_heads(query_grad), merge_heads(key_grad), merge_heads(value_grad))
    query_all, key_all, value_all = lax.map(one_sequence, (out_grad, queries, keys, values, keep_bits, query_later))
    return (query_all, key_all, value_all)
```

```python
import functools

import jax
import jax.numpy as jnp
from jax import lax
from jax.experimental import pallas as pl
from jax.experimental.pallas import tpu as pltpu
from jax.sharding import PartitionSpec as P

HD = 128
NC = 4
KT = 1024
FT = 256
MESH = pl.DeviceIdType.MESH
F32 = jnp.float32
BF = jnp.bfloat16


def dot_nt(a, b):
    return lax.dot_general(a, b, (((1,), (1,)), ((), ())), preferred_element_type=F32)


def dot_tn(a, b):
    return lax.dot_general(a, b, (((0,), (0,)), ((), ())), preferred_element_type=F32)


def dot_nn(a, b):
    return lax.dot_general(a, b, (((1,), (0,)), ((), ())), preferred_element_type=F32)


def split(start, count, size):
    return [(start + i, min(size, count - i)) for i in range(0, count, size)]


def kernel(
    n_seq, n_dp,
    og, w, q, k, v, kb, ql,
    qg, kg, vg,
    wbuf, g_own, g_rem, qb, kbuf, vb, kbits, qlb,
    gat, mk, ret, ks, kr, ki, ko, kbf, qs, qr, qi, qo, qaf, kgp, vgp, ob,
    ld, wsem, gsend, grecv, rsend, rrecv, kps, kpr, kcs, kcr, qps, qpr, qcs, qcr, osem,
):
    T, D = g_own.shape
    Wr = wbuf.shape[1]
    Fc = 2 * Wr
    Hc = Fc // HD
    X = n_dp // 2
    H = qb.shape[1] // HD
    R = T // NC
    n = lax.axis_index("seq")
    d = lax.axis_index("dp")
    x = d // 2
    c = lax.rem(d, 2)
    odd = lax.rem(n, 2)
    mate = n + 1 - 2 * odd
    has_lo = n >= 2
    has_hi = n < n_seq - 2
    core = (n, x * 2 + 1 - c)
    far = [(n, lax.rem(x + j, X) * 2 + c) for j in range(1, X)]

    barrier = pltpu.get_barrier_semaphore()
    for peer in [core, (mate, d)] + far:
        pl.semaphore_signal(barrier, inc=1, device_id=peer, device_id_type=MESH)

    @pl.when(has_lo)
    def _():
        pl.semaphore_signal(barrier, inc=1, device_id=(n - 2, d), device_id_type=MESH)

    @pl.when(has_hi)
    def _():
        pl.semaphore_signal(barrier, inc=1, device_id=(n + 2, d), device_id_type=MESH)

    loads = [
        pltpu.make_async_copy(k.at[0], kbuf, ld.at[0]),
        pltpu.make_async_copy(v.at[0], vb, ld.at[1]),
        pltpu.make_async_copy(kb.at[0], kbits, ld.at[2]),
        pltpu.make_async_copy(og.at[0], g_own, ld.at[3]),
        pltpu.make_async_copy(w, wbuf.at[c], ld.at[4]),
        pltpu.make_async_copy(q.at[0], qb, ld.at[5]),
        pltpu.make_async_copy(ql.at[0], qlb, ld.at[6]),
    ]
    for copy in loads:
        copy.start()
    pl.semaphore_wait(
        barrier, 1 + X + has_lo.astype(jnp.int32) + has_hi.astype(jnp.int32)
    )

    def remote(src, dst, ss, rs, dev):
        return pltpu.make_async_remote_copy(
            src_ref=src, dst_ref=dst, send_sem=ss, recv_sem=rs, device_id=dev, device_id_type=MESH
        )

    grad_copies = {}
    for i in range(NC):
        for j in range(1, X):
            s = X - 1 - j
            grad_copies[i, s] = remote(
                og.at[0, pl.ds(i * R, R), :], g_rem.at[s, pl.ds(i * R, R), :],
                gsend.at[i, j - 1], grecv.at[i, s], far[j - 1],
            )
            grad_copies[i, s].start()
    w_copy = remote(w, wbuf.at[c], wsem.at[0], wsem.at[1], core)
    w_copy.start()

    @pl.when(jnp.logical_not(has_lo))
    def _():
        ki[...] = jnp.zeros_like(ki)

    @pl.when(jnp.logical_not(has_hi))
    def _():
        qi[...] = jnp.zeros_like(qi)

    def lanes(h):
        return pl.ds(pl.multiple_of(h * HD, HD), HD)

    def head_of(j, hl):
        return lax.rem(x + j, X) * Hc + hl

    loads[0].wait()
    loads[1].wait()
    key_groups = split(0, H, 4)
    key_pair = []
    for gi, (p0, cnt) in enumerate(key_groups):
        @pl.loop(0, cnt)
        def _(i):
            h = p0 + i
            ks[h] = dot_tn(kbuf[:, lanes(h)], vb[:, lanes(h)]).astype(BF)

        copy = remote(ks.at[pl.ds(p0, cnt)], kr.at[pl.ds(p0, cnt)], kps.at[gi], kpr.at[gi], (mate, d))
        copy.start()
        key_pair.append(copy)

    loads[2].wait()
    words = kbits.shape[1]
    low = (kbits[...] & 255).astype(F32).astype(BF)
    high = (kbits[...] >> 8).astype(F32).astype(BF)
    row = lax.broadcasted_iota(jnp.int32, (words, HD), 0)
    lane = lax.broadcasted_iota(jnp.int32, (words, HD), 1)
    bit = lax.broadcasted_iota(jnp.int32, (T, HD), 1) & 7

    @pl.loop(0, H)
    def _(h):
        here = row == (lane >> 4) + h * 8
        first = (lane & 15) < 8
        pick_low = jnp.where(here & first, 1.0, 0.0).astype(BF)
        pick_high = jnp.where(here & jnp.logical_not(first), 1.0, 0.0).astype(BF)
        word = (dot_nn(low, pick_low) + dot_nn(high, pick_high)).astype(jnp.int32)
        mk[:, lanes(h)] = ((word >> bit) & 1).astype(F32).astype(BF)

    def project(g_ref, row0, rows, dst):
        pos = (n * T + row0 + lax.broadcasted_iota(jnp.int32, (rows, 1), 0)).astype(F32)
        scale = 2.0 / jnp.sqrt(HD * (pos + 1.0))
        for cc in range(2):
            @pl.loop(0, Wr // FT)
            def _(i):
                off = pl.multiple_of(i * FT, FT)
                acc = jnp.zeros((rows, FT), F32)
                for kk in range(0, D, KT):
                    acc = acc + dot_nt(
                        g_ref[pl.ds(row0, rows), pl.ds(kk, KT)],
                        wbuf[cc, pl.ds(off, FT), pl.ds(kk, KT)],
                    )
                dst[pl.ds(row0, rows), pl.ds(pl.multiple_of(cc * Wr + off, FT), FT)] = (
                    acc * scale
                ).astype(BF)

    def query_states(j, hl0, cnt):
        @pl.loop(0, cnt)
        def _(i):
            hl = hl0 + i
            h = head_of(j, hl)
            g = gat[j, :, lanes(hl)] * mk[:, lanes(h)]
            gat[j, :, lanes(hl)] = g
            qs[j * Hc + hl] = dot_tn(qb[:, lanes(h)], g).astype(BF)

    q_groups = []
    for j in range(X):
        for hl0, cnt in split(0, Hc, 4 if j == 0 else 2):
            q_groups.append((j, hl0, cnt))
    query_pair = {}

    def send_query_states(gi):
        j, hl0, cnt = q_groups[gi]
        query_states(j, hl0, cnt)
        rows = pl.ds(j * Hc + hl0, cnt)
        copy = remote(qs.at[rows], qr.at[rows], qps.at[gi], qpr.at[gi], (mate, d))
        copy.start()
        query_pair[gi] = copy

    def chain(gi, rows, pair, mine, got, inn, out, ss, rs, wait_if, send_if, to):
        pair.wait_recv()
        copy = remote(out.at[rows], inn.at[rows], ss.at[gi], rs.at[gi], to)

        @pl.when(wait_if)
        def _():
            copy.wait_recv()

        @pl.when(send_if)
        def _():
            out[rows] = (
                inn[rows].astype(F32) + (mine[rows].astype(F32) + got[rows].astype(F32))
            ).astype(BF)
            copy.start()

        return copy

    odd_f = odd.astype(F32)
    key_chain = []

    def key_step(gi):
        p0, cnt = key_groups[gi]
        rows = pl.ds(p0, cnt)
        to = (jnp.minimum(n + 2, n_seq - 2 + odd), d)
        key_chain.append(
            chain(gi, rows, key_pair[gi], ks, kr, ki, ko, kcs, kcr, has_lo, has_hi, to)
        )
        kbf[rows] = (ki[rows].astype(F32) + kr[rows].astype(F32) * odd_f).astype(BF)

    query_chain = []

    def query_step(gi):
        j, hl0, cnt = q_groups[gi]
        rows = pl.ds(j * Hc + hl0, cnt)
        to = (jnp.maximum(n - 2, odd), d)
        query_chain.append(
            chain(gi, rows, query_pair[gi], qs, qr, qi, qo, qcs, qcr, has_hi, has_lo, to)
        )

        @pl.loop(0, cnt)
        def _(i):
            p = j * Hc + hl0 + i
            h = head_of(j, hl0 + i)
            qaf[p] = (
                qlb[h] + (qi[p].astype(F32) + qr[p].astype(F32) * (1.0 - odd_f))
            ).astype(BF)

    tri = (
        lax.broadcasted_iota(jnp.int32, (T, T), 0) >= lax.broadcasted_iota(jnp.int32, (T, T), 1)
    )

    def inside(j):
        @pl.loop(0, Hc)
        def _(hl):
            h = head_of(j, hl)
            p = j * Hc + hl
            g = gat[j, :, lanes(hl)]
            qh, kh, vh = qb[:, lanes(h)], kbuf[:, lanes(h)], vb[:, lanes(h)]
            gs = jnp.where(tri, dot_nt(g, vh), 0.0).astype(BF)
            at = jnp.where(tri, dot_nt(qh, kh), 0.0).astype(BF)
            ob[0, :, lanes(h)] = (dot_nn(gs, kh) + dot_nt(g, kbf[h])).astype(BF)
            kgp[p] = dot_tn(gs, qh)
            vgp[p] = dot_tn(at, g)

    def across(j, hl0, cnt):
        @pl.loop(0, cnt)
        def _(i):
            hl = hl0 + i
            h = head_of(j, hl)
            p = j * Hc + hl
            qa = qaf[p]
            ob[1, :, lanes(h)] = (kgp[p] + dot_nt(vb[:, lanes(h)], qa)).astype(BF)
            ob[2, :, lanes(h)] = (vgp[p] + dot_nn(kbuf[:, lanes(h)], qa)).astype(BF)

    outs = []

    def store(o, j):
        cols = pl.ds(pl.multiple_of(lax.rem(x + j, X) * Fc, Fc), Fc)
        copy = pltpu.make_async_copy(
            ob.at[o, :, cols], (qg, kg, vg)[o].at[0, :, cols], osem.at[o, j]
        )
        copy.start()
        outs.append(copy)

    loads[3].wait()
    loads[4].wait()
    w_copy.wait_recv()
    project(g_own, 0, T, gat.at[0])
    loads[5].wait()
    loads[6].wait()
    local = [gi for gi, g in enumerate(q_groups) if g[0] == 0]
    distant = [gi for gi, g in enumerate(q_groups) if g[0] > 0]
    for gi in local:
        send_query_states(gi)
    for gi in range(len(key_groups)):
        key_step(gi)

    ret_copies = []

    def serve(i):
        for s in range(X - 1):
            grad_copies[i, s].wait_recv()
            project(g_rem.at[s], i * R, R, ret.at[s])
            back = X - 1 - s
            copy = remote(
                ret.at[s, pl.ds(i * R, R), :], gat.at[back, pl.ds(i * R, R), :],
                rsend.at[i, s], rrecv.at[i, back - 1], far[s],
            )
            copy.start()
            ret_copies.append(copy)

    serve(0)
    for gi in local:
        query_step(gi)
    inside(0)
    store(0, 0)
    serve(1)
    for gi in local:
        across(*q_groups[gi])
    store(1, 0)
    store(2, 0)
    for i in range(2, NC):
        serve(i)
    for copy in ret_copies:
        copy.wait_recv()
    for gi in distant:
        send_query_states(gi)
    for j in range(1, X):
        inside(j)
        store(0, j)
    for gi in distant:
        query_step(gi)
        across(*q_groups[gi])
    for j in range(1, X):
        store(1, j)
        store(2, j)

    for copy in list(grad_copies.values()) + [w_copy] + ret_copies + key_pair:
        copy.wait_send()
    for copy in query_pair.values():
        copy.wait_send()

    @pl.when(has_hi)
    def _():
        for copy in key_chain:
            copy.wait_send()

    @pl.when(has_lo)
    def _():
        for copy in query_chain:
            copy.wait_send()

    for copy in outs:
        copy.wait()


def body(n_seq, n_dp, out_grad, w_out, queries, keys, values, keep_bits, query_later):
    T, D = out_grad.shape[1:]
    I = queries.shape[2]
    Wr = w_out.shape[0]
    Fc = 2 * Wr
    Hc = Fc // HD
    X = n_dp // 2
    H = I // HD
    kgn = len(split(0, H, 4))
    qgn = len(split(0, Hc, 4)) + (X - 1) * len(split(0, Hc, 2))
    state = pltpu.VMEM((H, HD, HD), BF)
    dma = pltpu.SemaphoreType.DMA
    far = max(X - 1, 1)
    scratch = [
        pltpu.VMEM((2, Wr, D), BF),
        pltpu.VMEM((T, D), BF),
        pltpu.VMEM((far, T, D), BF),
        pltpu.VMEM((T, I), BF),
        pltpu.VMEM((T, I), BF),
        pltpu.VMEM((T, I), BF),
        pltpu.VMEM((T, keep_bits.shape[2]), jnp.int32),
        pltpu.VMEM((H, HD, HD), F32),
        pltpu.VMEM((X, T, Fc), BF),
        pltpu.VMEM((T, I), BF),
        pltpu.VMEM((far, T, Fc), BF),
        state, state, state, state, state,
        state, state, state, state, state,
        pltpu.VMEM((H, T, HD), F32),
        pltpu.VMEM((H, T, HD), F32),
        pltpu.VMEM((3, T, I), BF),
        dma((7,)), dma((2,)),
        dma((NC, far)), dma((NC, far)), dma((NC, far)), dma((NC, far)),
        dma((kgn,)), dma((kgn,)), dma((kgn,)), dma((kgn,)),
        dma((qgn,)), dma((qgn,)), dma((qgn,)), dma((qgn,)),
        dma((3, X)),
    ]
    out = jax.ShapeDtypeStruct((1, T, I), BF)
    hbm = pl.BlockSpec(memory_space=pl.ANY)
    return pl.pallas_call(
        functools.partial(kernel, n_seq, n_dp),
        out_shape=(out, out, out),
        in_specs=[hbm] * 7,
        out_specs=(hbm, hbm, hbm),
        scratch_shapes=scratch,
        compiler_params=pltpu.CompilerParams(
            collective_id=0, has_side_effects=True, vmem_limit_bytes=60 * 1024 * 1024
        ),
    )(out_grad, w_out, queries, keys, values, keep_bits, query_later)


def solution(mesh):
    rows = P("dp", "seq", None)
    in_specs = (rows, P("dp", None), rows, rows, rows, rows, P("dp", None, None, None))
    fn = functools.partial(body, mesh.shape["seq"], mesh.shape["dp"])
    return jax.shard_map(fn, mesh=mesh, in_specs=in_specs, out_specs=(rows, rows, rows), check_vma=False)
```

```python
import functools

import jax
import jax.numpy as jnp
from jax import lax
from jax.experimental import pallas as pl
from jax.experimental.pallas import tpu as pltpu
from jax.sharding import PartitionSpec as P

HD = 128
NC = 4
KT = 1024
FT = 256
MESH = pl.DeviceIdType.MESH
F32 = jnp.float32
BF = jnp.bfloat16


def dot_nt(a, b):
    return lax.dot_general(a, b, (((1,), (1,)), ((), ())), preferred_element_type=F32)


def dot_tn(a, b):
    return lax.dot_general(a, b, (((0,), (0,)), ((), ())), preferred_element_type=F32)


def dot_nn(a, b):
    return lax.dot_general(a, b, (((1,), (0,)), ((), ())), preferred_element_type=F32)


def split(start, count, size):
    return [(start + i, min(size, count - i)) for i in range(0, count, size)]


def kernel(
    n_seq, n_dp,
    og, w, q, k, v, kb, ql,
    qg, kg, vg,
    wbuf, g_own, g_rem, qb, kbuf, vb, kbits, qlb,
    gat, mk, ret, ks, kr, ki, ko, kbf, qs, qr, qi, qo, qaf, qgp, kgp, vgp, ob,
    ld, wsem, gsend, grecv, rsend, rrecv, kps, kpr, kcs, kcr, qps, qpr, qcs, qcr, osem,
):
    T, D = g_own.shape
    Wr = wbuf.shape[1]
    Fc = 2 * Wr
    Hc = Fc // HD
    X = n_dp // 2
    H = qb.shape[1] // HD
    R = T // NC
    n = lax.axis_index("seq")
    d = lax.axis_index("dp")
    x = d // 2
    c = lax.rem(d, 2)
    odd = lax.rem(n, 2)
    mate = n + 1 - 2 * odd
    level = n // 2
    back_level = n_seq // 2 - 1 - level
    has_lo = n >= 2
    has_hi = n < n_seq - 2
    core = (n, x * 2 + 1 - c)
    far = [(n, lax.rem(x + j, X) * 2 + c) for j in range(1, X)]

    barrier = pltpu.get_barrier_semaphore()
    for peer in [core, (mate, d)] + far:
        pl.semaphore_signal(barrier, inc=1, device_id=peer, device_id_type=MESH)

    @pl.when(has_lo)
    def _():
        pl.semaphore_signal(barrier, inc=1, device_id=(n - 2, d), device_id_type=MESH)

    @pl.when(has_hi)
    def _():
        pl.semaphore_signal(barrier, inc=1, device_id=(n + 2, d), device_id_type=MESH)

    loads = [
        pltpu.make_async_copy(k.at[0], kbuf, ld.at[0]),
        pltpu.make_async_copy(v.at[0], vb, ld.at[1]),
        pltpu.make_async_copy(kb.at[0], kbits, ld.at[2]),
        pltpu.make_async_copy(og.at[0], g_own, ld.at[3]),
        pltpu.make_async_copy(w, wbuf.at[c], ld.at[4]),
        pltpu.make_async_copy(q.at[0], qb, ld.at[5]),
        pltpu.make_async_copy(ql.at[0], qlb, ld.at[6]),
    ]
    for copy in loads:
        copy.start()
    pl.semaphore_wait(
        barrier, 1 + X + has_lo.astype(jnp.int32) + has_hi.astype(jnp.int32)
    )

    def remote(src, dst, ss, rs, dev):
        return pltpu.make_async_remote_copy(
            src_ref=src, dst_ref=dst, send_sem=ss, recv_sem=rs, device_id=dev, device_id_type=MESH
        )

    grad_copies = {}
    for i in range(NC):
        for j in range(1, X):
            s = X - 1 - j
            grad_copies[i, s] = remote(
                og.at[0, pl.ds(i * R, R), :], g_rem.at[s, pl.ds(i * R, R), :],
                gsend.at[i, j - 1], grecv.at[i, s], far[j - 1],
            )
            grad_copies[i, s].start()
    w_copy = remote(w, wbuf.at[c], wsem.at[0], wsem.at[1], core)
    w_copy.start()

    @pl.when(jnp.logical_not(has_lo))
    def _():
        ki[...] = jnp.zeros_like(ki)

    @pl.when(jnp.logical_not(has_hi))
    def _():
        qi[...] = jnp.zeros_like(qi)

    def lanes(h):
        return pl.ds(pl.multiple_of(h * HD, HD), HD)

    def head_of(j, hl):
        return lax.rem(x + j, X) * Hc + hl

    loads[0].wait()
    loads[1].wait()
    key_groups = split(0, H, 4)
    key_pair = []
    for gi, (p0, cnt) in enumerate(key_groups):
        @pl.loop(0, cnt)
        def _(i):
            h = p0 + i
            ks[h] = dot_tn(kbuf[:, lanes(h)], vb[:, lanes(h)]).astype(BF)

        copy = remote(ks.at[pl.ds(p0, cnt)], kr.at[pl.ds(p0, cnt)], kps.at[gi], kpr.at[gi], (mate, d))
        copy.start()
        key_pair.append(copy)

    loads[2].wait()
    words = kbits.shape[1]
    low = (kbits[...] & 255).astype(F32).astype(BF)
    high = (kbits[...] >> 8).astype(F32).astype(BF)
    row = lax.broadcasted_iota(jnp.int32, (words, HD), 0)
    lane = lax.broadcasted_iota(jnp.int32, (words, HD), 1)
    bit = lax.broadcasted_iota(jnp.int32, (T, HD), 1) & 7

    @pl.loop(0, H)
    def _(h):
        here = row == (lane >> 4) + h * 8
        first = (lane & 15) < 8
        pick_low = jnp.where(here & first, 1.0, 0.0).astype(BF)
        pick_high = jnp.where(here & jnp.logical_not(first), 1.0, 0.0).astype(BF)
        word = (dot_nn(low, pick_low) + dot_nn(high, pick_high)).astype(jnp.int32)
        mk[:, lanes(h)] = ((word >> bit) & 1).astype(F32).astype(BF)

    def project(g_ref, row0, rows, dst, halves):
        pos = (n * T + row0 + lax.broadcasted_iota(jnp.int32, (rows, 1), 0)).astype(F32)
        scale = 2.0 / jnp.sqrt(HD * (pos + 1.0))
        for cc in halves:
            @pl.loop(0, Wr // FT)
            def _(i):
                off = pl.multiple_of(i * FT, FT)
                acc = jnp.zeros((rows, FT), F32)
                for kk in range(0, D, KT):
                    acc = acc + dot_nt(
                        g_ref[pl.ds(row0, rows), pl.ds(kk, KT)],
                        wbuf[cc, pl.ds(off, FT), pl.ds(kk, KT)],
                    )
                dst[pl.ds(row0, rows), pl.ds(pl.multiple_of(cc * Wr + off, FT), FT)] = (
                    acc * scale
                ).astype(BF)

    def query_states(j, hl0, cnt):
        @pl.loop(0, cnt)
        def _(i):
            hl = hl0 + i
            h = head_of(j, hl)
            g = gat[j, :, lanes(hl)] * mk[:, lanes(h)]
            gat[j, :, lanes(hl)] = g
            qs[j * Hc + hl] = dot_tn(qb[:, lanes(h)], g).astype(BF)

    q_groups = []
    for j in range(X):
        for hl0, cnt in split(0, Hc, 4 if j == 0 else 2):
            q_groups.append((j, hl0, cnt))
    query_pair = {}

    def send_query_states(gi):
        j, hl0, cnt = q_groups[gi]
        query_states(j, hl0, cnt)
        rows = pl.ds(j * Hc + hl0, cnt)
        copy = remote(qs.at[rows], qr.at[rows], qps.at[gi], qpr.at[gi], (mate, d))
        copy.start()
        query_pair[gi] = copy

    def chain(rows, copy, pair, mine, got, inn, out, wait_if, send_if):
        pair.wait_recv()

        @pl.when(wait_if)
        def _():
            copy.wait_recv()

        @pl.when(send_if)
        def _():
            out[rows] = (
                inn[rows].astype(F32) + (mine[rows].astype(F32) + got[rows].astype(F32))
            ).astype(BF)
            copy.start()

    odd_f = odd.astype(F32)

    def key_copy(gi):
        p0, cnt = key_groups[gi]
        rows = pl.ds(p0, cnt)
        to = (jnp.minimum(n + 2, n_seq - 2 + odd), d)
        return rows, remote(ko.at[rows], ki.at[rows], kcs.at[gi], kcr.at[gi], to)

    def query_copy(gi):
        j, hl0, cnt = q_groups[gi]
        rows = pl.ds(j * Hc + hl0, cnt)
        to = (jnp.maximum(n - 2, odd), d)
        return rows, remote(qo.at[rows], qi.at[rows], qcs.at[gi], qcr.at[gi], to)

    def key_step(gi):
        rows, copy = key_copy(gi)
        chain(rows, copy, key_pair[gi], ks, kr, ki, ko, has_lo, has_hi)
        kbf[rows] = (ki[rows].astype(F32) + kr[rows].astype(F32) * odd_f).astype(BF)

    def query_step(gi):
        rows, copy = query_copy(gi)
        chain(rows, copy, query_pair[gi], qs, qr, qi, qo, has_hi, has_lo)
        j, hl0, cnt = q_groups[gi]

        @pl.loop(0, cnt)
        def _(i):
            p = j * Hc + hl0 + i
            h = head_of(j, hl0 + i)
            qaf[p] = (
                qlb[h] + (qi[p].astype(F32) + qr[p].astype(F32) * (1.0 - odd_f))
            ).astype(BF)

    tri = (
        lax.broadcasted_iota(jnp.int32, (T, T), 0) >= lax.broadcasted_iota(jnp.int32, (T, T), 1)
    )

    def inside(j):
        @pl.loop(0, Hc)
        def _(hl):
            h = head_of(j, hl)
            p = j * Hc + hl
            g = gat[j, :, lanes(hl)]
            qh, kh, vh = qb[:, lanes(h)], kbuf[:, lanes(h)], vb[:, lanes(h)]
            gs = jnp.where(tri, dot_nt(g, vh), 0.0).astype(BF)
            at = jnp.where(tri, dot_nt(qh, kh), 0.0).astype(BF)
            qgp[p] = dot_nn(gs, kh)
            kgp[p] = dot_tn(gs, qh)
            vgp[p] = dot_tn(at, g)

    def across_k():
        for j in range(X):
            @pl.loop(0, Hc)
            def _(hl):
                h = head_of(j, hl)
                ob[0, :, lanes(h)] = (
                    qgp[j * Hc + hl] + dot_nt(gat[j, :, lanes(hl)], kbf[h])
                ).astype(BF)

    def across_q(j, hl0, cnt):
        @pl.loop(0, cnt)
        def _(i):
            hl = hl0 + i
            h = head_of(j, hl)
            p = j * Hc + hl
            qa = qaf[p]
            ob[1, :, lanes(h)] = (kgp[p] + dot_nt(vb[:, lanes(h)], qa)).astype(BF)
            ob[2, :, lanes(h)] = (vgp[p] + dot_nn(kbuf[:, lanes(h)], qa)).astype(BF)

    outs = []

    def store(o, j):
        cols = pl.ds(pl.multiple_of(lax.rem(x + j, X) * Fc, Fc), Fc)
        copy = pltpu.make_async_copy(
            ob.at[o, :, cols], (qg, kg, vg)[o].at[0, :, cols], osem.at[o, j]
        )
        copy.start()
        outs.append(copy)

    local = [gi for gi, g in enumerate(q_groups) if g[0] == 0]
    distant = [gi for gi, g in enumerate(q_groups) if g[0] > 0]

    def slot(place, number):
        return place >= number if number == 3 else place == number

    def key_slot(number):
        @pl.when(slot(level, number))
        def _():
            for gi in range(len(key_groups)):
                key_step(gi)

    def query_slot(number):
        @pl.when(slot(back_level, number))
        def _():
            for gi in local:
                query_step(gi)

    loads[3].wait()
    loads[4].wait()
    project(g_own, 0, T, gat.at[0], [c])
    w_copy.wait_recv()
    project(g_own, 0, T, gat.at[0], [1 - c])
    loads[5].wait()
    loads[6].wait()
    for gi in local:
        send_query_states(gi)
    key_slot(0)

    ret_copies = []

    def serve(i):
        for s in range(X - 1):
            grad_copies[i, s].wait_recv()
            project(g_rem.at[s], i * R, R, ret.at[s], [0, 1])
            back = X - 1 - s
            copy = remote(
                ret.at[s, pl.ds(i * R, R), :], gat.at[back, pl.ds(i * R, R), :],
                rsend.at[i, s], rrecv.at[i, back - 1], far[s],
            )
            copy.start()
            ret_copies.append(copy)

    serve(0)
    query_slot(0)
    serve(1)
    inside(0)
    key_slot(1)
    query_slot(1)
    for i in range(2, NC):
        serve(i)
    key_slot(2)
    query_slot(2)
    for copy in ret_copies:
        copy.wait_recv()
    for gi in distant:
        send_query_states(gi)
    query_slot(3)
    for j in range(1, X):
        inside(j)
    for gi in local:
        across_q(*q_groups[gi])
    store(1, 0)
    store(2, 0)

    @pl.when(level < 3)
    def _():
        across_k()

    for gi in distant:
        query_step(gi)
        across_q(*q_groups[gi])
    for j in range(1, X):
        store(1, j)
        store(2, j)
    key_slot(3)

    @pl.when(level >= 3)
    def _():
        across_k()

    for j in range(X):
        store(0, j)

    for copy in list(grad_copies.values()) + [w_copy] + ret_copies + key_pair:
        copy.wait_send()
    for copy in query_pair.values():
        copy.wait_send()

    @pl.when(has_hi)
    def _():
        for gi in range(len(key_groups)):
            key_copy(gi)[1].wait_send()

    @pl.when(has_lo)
    def _():
        for gi in range(len(q_groups)):
            query_copy(gi)[1].wait_send()

    for copy in outs:
        copy.wait()


def settle(a, b, c, oa, ob, oc, buf, isem, osem):
    rows = buf.shape[1] // 2
    pairs = []
    for o, (src, dst) in enumerate(((a, oa), (b, ob), (c, oc))):
        for i in range(2):
            part = pl.ds(i * rows, rows)
            into = pltpu.make_async_copy(src.at[0, part], buf.at[o, part], isem.at[o, i])
            into.start()
            pairs.append((into, pltpu.make_async_copy(buf.at[o, part], dst.at[0, part], osem.at[o, i])))
    for into, out in pairs:
        into.wait()
        out.start()
    for _, out in pairs:
        out.wait()


def body(n_seq, n_dp, out_grad, w_out, queries, keys, values, keep_bits, query_later):
    T, D = out_grad.shape[1:]
    I = queries.shape[2]
    Wr = w_out.shape[0]
    Fc = 2 * Wr
    Hc = Fc // HD
    X = n_dp // 2
    H = I // HD
    kgn = len(split(0, H, 4))
    qgn = len(split(0, Hc, 4)) + (X - 1) * len(split(0, Hc, 2))
    state = pltpu.VMEM((H, HD, HD), BF)
    dma = pltpu.SemaphoreType.DMA
    far = max(X - 1, 1)
    scratch = [
        pltpu.VMEM((2, Wr, D), BF),
        pltpu.VMEM((T, D), BF),
        pltpu.VMEM((far, T, D), BF),
        pltpu.VMEM((T, I), BF),
        pltpu.VMEM((T, I), BF),
        pltpu.VMEM((T, I), BF),
        pltpu.VMEM((T, keep_bits.shape[2]), jnp.int32),
        pltpu.VMEM((H, HD, HD), F32),
        pltpu.VMEM((X, T, Fc), BF),
        pltpu.VMEM((T, I), BF),
        pltpu.VMEM((far, T, Fc), BF),
        state, state, state, state, state,
        state, state, state, state, state,
        pltpu.VMEM((H, T, HD), F32),
        pltpu.VMEM((H, T, HD), F32),
        pltpu.VMEM((H, T, HD), F32),
        pltpu.VMEM((3, T, I), BF),
        dma((7,)), dma((2,)),
        dma((NC, far)), dma((NC, far)), dma((NC, far)), dma((NC, far)),
        dma((kgn,)), dma((kgn,)), dma((kgn,)), dma((kgn,)),
        dma((qgn,)), dma((qgn,)), dma((qgn,)), dma((qgn,)),
        dma((3, X)),
    ]
    out = jax.ShapeDtypeStruct((1, T, I), BF)
    hbm = pl.BlockSpec(memory_space=pl.ANY)
    parts = pl.pallas_call(
        functools.partial(kernel, n_seq, n_dp),
        out_shape=(out, out, out),
        in_specs=[hbm] * 7,
        out_specs=(hbm, hbm, hbm),
        scratch_shapes=scratch,
        compiler_params=pltpu.CompilerParams(
            collective_id=0, has_side_effects=True, vmem_limit_bytes=60 * 1024 * 1024
        ),
    )(out_grad, w_out, queries, keys, values, keep_bits, query_later)
    return pl.pallas_call(
        settle,
        out_shape=(out, out, out),
        in_specs=[hbm] * 3,
        out_specs=(hbm, hbm, hbm),
        scratch_shapes=[pltpu.VMEM((3, T, I), BF), dma((3, 2)), dma((3, 2))],
    )(*parts)


def solution(mesh):
    rows = P("dp", "seq", None)
    in_specs = (rows, P("dp", None), rows, rows, rows, rows, P("dp", None, None, None))
    fn = functools.partial(body, mesh.shape["seq"], mesh.shape["dp"])
    return jax.shard_map(fn, mesh=mesh, in_specs=in_specs, out_specs=(rows, rows, rows), check_vma=False)
```

```python
import functools

import jax
import jax.numpy as jnp
from jax import lax
from jax.experimental import pallas as pl
from jax.experimental.pallas import tpu as pltpu
from jax.sharding import PartitionSpec as P

HD = 128
NC = 4
KT = 1024
FT = 256
MESH = pl.DeviceIdType.MESH
F32 = jnp.float32
BF = jnp.bfloat16


def dot_nt(a, b):
    return lax.dot_general(a, b, (((1,), (1,)), ((), ())), preferred_element_type=F32)


def dot_tn(a, b):
    return lax.dot_general(a, b, (((0,), (0,)), ((), ())), preferred_element_type=F32)


def dot_nn(a, b):
    return lax.dot_general(a, b, (((1,), (0,)), ((), ())), preferred_element_type=F32)


def split(start, count, size):
    return [(start + i, min(size, count - i)) for i in range(0, count, size)]


def kernel(
    n_seq, n_dp,
    og, w, q, k, v, kb, ql,
    qg, kg, vg,
    wbuf, g_own, g_rem, qb, kbuf, vb, kbits, qlb,
    gat, mk, ret, ks, kr, ki, ko, kbf, qs, qr, qi, qo, qaf, qgp, kgp, vgp, ob,
    ld, wsem, gsend, grecv, rsend, rrecv, kps, kpr, kcs, kcr, qps, qpr, qcs, qcr, osem,
):
    T, D = g_own.shape
    Wr = wbuf.shape[1]
    Fc = 2 * Wr
    Hc = Fc // HD
    X = n_dp // 2
    H = qb.shape[1] // HD
    R = T // NC
    n = lax.axis_index("seq")
    d = lax.axis_index("dp")
    x = d // 2
    c = lax.rem(d, 2)
    odd = lax.rem(n, 2)
    mate = n + 1 - 2 * odd
    level = n // 2
    back_level = n_seq // 2 - 1 - level
    has_lo = n >= 2
    has_hi = n < n_seq - 2
    core = (n, x * 2 + 1 - c)
    far = [(n, lax.rem(x + j, X) * 2 + c) for j in range(1, X)]

    barrier = pltpu.get_barrier_semaphore()
    for peer in [core, (mate, d)] + far:
        pl.semaphore_signal(barrier, inc=1, device_id=peer, device_id_type=MESH)

    @pl.when(has_lo)
    def _():
        pl.semaphore_signal(barrier, inc=1, device_id=(n - 2, d), device_id_type=MESH)

    @pl.when(has_hi)
    def _():
        pl.semaphore_signal(barrier, inc=1, device_id=(n + 2, d), device_id_type=MESH)

    loads = [
        pltpu.make_async_copy(k.at[0], kbuf, ld.at[0]),
        pltpu.make_async_copy(v.at[0], vb, ld.at[1]),
        pltpu.make_async_copy(kb.at[0], kbits, ld.at[2]),
        pltpu.make_async_copy(og.at[0], g_own, ld.at[3]),
        pltpu.make_async_copy(w, wbuf.at[c], ld.at[4]),
        pltpu.make_async_copy(q.at[0], qb, ld.at[5]),
        pltpu.make_async_copy(ql.at[0], qlb, ld.at[6]),
    ]
    for copy in loads:
        copy.start()
    pl.semaphore_wait(
        barrier, 1 + X + has_lo.astype(jnp.int32) + has_hi.astype(jnp.int32)
    )

    def remote(src, dst, ss, rs, dev):
        return pltpu.make_async_remote_copy(
            src_ref=src, dst_ref=dst, send_sem=ss, recv_sem=rs, device_id=dev, device_id_type=MESH
        )

    grad_copies = {}
    for i in range(NC):
        for j in range(1, X):
            s = X - 1 - j
            grad_copies[i, s] = remote(
                og.at[0, pl.ds(i * R, R), :], g_rem.at[s, pl.ds(i * R, R), :],
                gsend.at[i, j - 1], grecv.at[i, s], far[j - 1],
            )
            grad_copies[i, s].start()
    w_copy = remote(w, wbuf.at[c], wsem.at[0], wsem.at[1], core)
    w_copy.start()

    @pl.when(jnp.logical_not(has_lo))
    def _():
        ki[...] = jnp.zeros_like(ki)

    @pl.when(jnp.logical_not(has_hi))
    def _():
        qi[...] = jnp.zeros_like(qi)

    def lanes(h):
        return pl.ds(pl.multiple_of(h * HD, HD), HD)

    def head_of(j, hl):
        return lax.rem(x + j, X) * Hc + hl

    loads[0].wait()
    loads[1].wait()
    key_groups = split(0, H, 4)
    key_pair = []
    for gi, (p0, cnt) in enumerate(key_groups):
        @pl.loop(0, cnt)
        def _(i):
            h = p0 + i
            ks[h] = dot_tn(kbuf[:, lanes(h)], vb[:, lanes(h)]).astype(BF)

        copy = remote(ks.at[pl.ds(p0, cnt)], kr.at[pl.ds(p0, cnt)], kps.at[gi], kpr.at[gi], (mate, d))
        copy.start()
        key_pair.append(copy)

    loads[2].wait()
    words = kbits.shape[1]
    low = (kbits[...] & 255).astype(F32).astype(BF)
    high = (kbits[...] >> 8).astype(F32).astype(BF)
    row = lax.broadcasted_iota(jnp.int32, (words, HD), 0)
    lane = lax.broadcasted_iota(jnp.int32, (words, HD), 1)
    bit = lax.broadcasted_iota(jnp.int32, (T, HD), 1) & 7

    @pl.loop(0, H)
    def _(h):
        here = row == (lane >> 4) + h * 8
        first = (lane & 15) < 8
        pick_low = jnp.where(here & first, 1.0, 0.0).astype(BF)
        pick_high = jnp.where(here & jnp.logical_not(first), 1.0, 0.0).astype(BF)
        word = (dot_nn(low, pick_low) + dot_nn(high, pick_high)).astype(jnp.int32)
        mk[:, lanes(h)] = ((word >> bit) & 1).astype(F32).astype(BF)

    def project(g_ref, row0, rows, dst, halves):
        pos = (n * T + row0 + lax.broadcasted_iota(jnp.int32, (rows, 1), 0)).astype(F32)
        scale = 2.0 / jnp.sqrt(HD * (pos + 1.0))
        for cc in halves:
            @pl.loop(0, Wr // FT)
            def _(i):
                off = pl.multiple_of(i * FT, FT)
                acc = jnp.zeros((rows, FT), F32)
                for kk in range(0, D, KT):
                    acc = acc + dot_nt(
                        g_ref[pl.ds(row0, rows), pl.ds(kk, KT)],
                        wbuf[cc, pl.ds(off, FT), pl.ds(kk, KT)],
                    )
                dst[pl.ds(row0, rows), pl.ds(pl.multiple_of(cc * Wr + off, FT), FT)] = (
                    acc * scale
                ).astype(BF)

    def query_states(j, hl0, cnt):
        @pl.loop(0, cnt)
        def _(i):
            hl = hl0 + i
            h = head_of(j, hl)
            g = gat[j, :, lanes(hl)] * mk[:, lanes(h)]
            gat[j, :, lanes(hl)] = g
            qs[j * Hc + hl] = dot_tn(qb[:, lanes(h)], g).astype(BF)

    q_groups = []
    for j in range(X):
        for hl0, cnt in split(0, Hc, 4 if j == 0 else 1):
            q_groups.append((j, hl0, cnt))
    query_pair = {}

    def send_query_states(gi):
        j, hl0, cnt = q_groups[gi]
        query_states(j, hl0, cnt)
        rows = pl.ds(j * Hc + hl0, cnt)
        copy = remote(qs.at[rows], qr.at[rows], qps.at[gi], qpr.at[gi], (mate, d))
        copy.start()
        query_pair[gi] = copy

    def chain(rows, copy, pair, mine, got, inn, out, wait_if, send_if):
        pair.wait_recv()

        @pl.when(wait_if)
        def _():
            copy.wait_recv()

        @pl.when(send_if)
        def _():
            out[rows] = (
                inn[rows].astype(F32) + (mine[rows].astype(F32) + got[rows].astype(F32))
            ).astype(BF)
            copy.start()

    odd_f = odd.astype(F32)

    def key_copy(gi):
        p0, cnt = key_groups[gi]
        rows = pl.ds(p0, cnt)
        to = (jnp.minimum(n + 2, n_seq - 2 + odd), d)
        return rows, remote(ko.at[rows], ki.at[rows], kcs.at[gi], kcr.at[gi], to)

    def query_copy(gi):
        j, hl0, cnt = q_groups[gi]
        rows = pl.ds(j * Hc + hl0, cnt)
        to = (jnp.maximum(n - 2, odd), d)
        return rows, remote(qo.at[rows], qi.at[rows], qcs.at[gi], qcr.at[gi], to)

    def key_step(gi):
        rows, copy = key_copy(gi)
        chain(rows, copy, key_pair[gi], ks, kr, ki, ko, has_lo, has_hi)
        kbf[rows] = (ki[rows].astype(F32) + kr[rows].astype(F32) * odd_f).astype(BF)

    def query_step(gi):
        rows, copy = query_copy(gi)
        chain(rows, copy, query_pair[gi], qs, qr, qi, qo, has_hi, has_lo)
        j, hl0, cnt = q_groups[gi]

        @pl.loop(0, cnt)
        def _(i):
            p = j * Hc + hl0 + i
            h = head_of(j, hl0 + i)
            qaf[p] = (
                qlb[h] + (qi[p].astype(F32) + qr[p].astype(F32) * (1.0 - odd_f))
            ).astype(BF)

    tri = (
        lax.broadcasted_iota(jnp.int32, (T, T), 0) >= lax.broadcasted_iota(jnp.int32, (T, T), 1)
    )

    def inside(j, hl0, cnt):
        @pl.loop(0, cnt)
        def _(i):
            hl = hl0 + i
            h = head_of(j, hl)
            p = j * Hc + hl
            g = gat[j, :, lanes(hl)]
            qh, kh, vh = qb[:, lanes(h)], kbuf[:, lanes(h)], vb[:, lanes(h)]
            gs = jnp.where(tri, dot_nt(g, vh), 0.0).astype(BF)
            at = jnp.where(tri, dot_nt(qh, kh), 0.0).astype(BF)
            qgp[p] = dot_nn(gs, kh)
            kgp[p] = dot_tn(gs, qh)
            vgp[p] = dot_tn(at, g)

    def across_k():
        for j in range(X):
            @pl.loop(0, Hc)
            def _(hl):
                h = head_of(j, hl)
                ob[0, :, lanes(h)] = (
                    qgp[j * Hc + hl] + dot_nt(gat[j, :, lanes(hl)], kbf[h])
                ).astype(BF)

    def across_q(j, hl0, cnt):
        @pl.loop(0, cnt)
        def _(i):
            hl = hl0 + i
            h = head_of(j, hl)
            p = j * Hc + hl
            qa = qaf[p]
            ob[1, :, lanes(h)] = (kgp[p] + dot_nt(vb[:, lanes(h)], qa)).astype(BF)
            ob[2, :, lanes(h)] = (vgp[p] + dot_nn(kbuf[:, lanes(h)], qa)).astype(BF)

    outs = []

    def store(o, j):
        cols = pl.ds(pl.multiple_of(lax.rem(x + j, X) * Fc, Fc), Fc)
        copy = pltpu.make_async_copy(
            ob.at[o, :, cols], (qg, kg, vg)[o].at[0, :, cols], osem.at[o, j]
        )
        copy.start()
        outs.append(copy)

    local = [gi for gi, g in enumerate(q_groups) if g[0] == 0]
    distant = [gi for gi, g in enumerate(q_groups) if g[0] > 0]

    def slot(place, number):
        return place >= number if number == 3 else place == number

    def key_slot(number):
        @pl.when(slot(level, number))
        def _():
            for gi in range(len(key_groups)):
                key_step(gi)

    def query_slot(number):
        @pl.when(slot(back_level, number))
        def _():
            for gi in local:
                query_step(gi)

    loads[3].wait()
    loads[4].wait()
    project(g_own, 0, T, gat.at[0], [c])
    w_copy.wait_recv()
    project(g_own, 0, T, gat.at[0], [1 - c])
    loads[5].wait()
    loads[6].wait()
    for gi in local:
        send_query_states(gi)
    key_slot(0)

    ret_copies = ([], [])

    def give_back(cc, i, s, row0, rows):
        back = X - 1 - s
        part = (pl.ds(row0, rows), pl.ds(cc * Wr, Wr))
        copy = remote(
            ret.at[(s, *part)], gat.at[(back, *part)],
            rsend.at[cc, i, s], rrecv.at[cc, i, back - 1], far[s],
        )
        copy.start()
        ret_copies[cc].append(copy)

    def serve(i):
        for s in range(X - 1):
            grad_copies[i, s].wait_recv()
            project(g_rem.at[s], i * R, R, ret.at[s], [0])
            give_back(0, i, s, i * R, R)
            if i == NC - 1:
                give_back(1, 0, s, 0, i * R)
            project(g_rem.at[s], i * R, R, ret.at[s], [1])
            if i == NC - 1:
                give_back(1, 1, s, i * R, R)

    half = Hc // 2
    distant = [[gi for gi in distant if (q_groups[gi][1] >= half) == late] for late in (False, True)]
    serve(0)
    query_slot(0)
    serve(1)
    inside(0, 0, Hc)
    key_slot(1)
    query_slot(1)
    for i in range(2, NC):
        serve(i)
    key_slot(2)
    query_slot(2)
    for copy in ret_copies[0]:
        copy.wait_recv()
    for gi in distant[0]:
        send_query_states(gi)
    query_slot(3)
    for j in range(1, X):
        inside(j, 0, half)
    for gi in local:
        across_q(*q_groups[gi])
    store(1, 0)
    store(2, 0)
    for copy in ret_copies[1]:
        copy.wait_recv()
    for gi in distant[1]:
        send_query_states(gi)
    for j in range(1, X):
        inside(j, half, Hc - half)

    @pl.when(level < 3)
    def _():
        across_k()

    for gi in distant[0] + distant[1]:
        query_step(gi)
        across_q(*q_groups[gi])
    for j in range(1, X):
        store(1, j)
        store(2, j)
    key_slot(3)

    @pl.when(level >= 3)
    def _():
        across_k()

    for j in range(X):
        store(0, j)

    for copy in list(grad_copies.values()) + [w_copy] + ret_copies[0] + ret_copies[1] + key_pair:
        copy.wait_send()
    for copy in query_pair.values():
        copy.wait_send()

    @pl.when(has_hi)
    def _():
        for gi in range(len(key_groups)):
            key_copy(gi)[1].wait_send()

    @pl.when(has_lo)
    def _():
        for gi in range(len(q_groups)):
            query_copy(gi)[1].wait_send()

    for copy in outs:
        copy.wait()


def settle(a, b, c, oa, ob, oc, buf, isem, osem):
    rows = buf.shape[1] // 2
    pairs = []
    for o, (src, dst) in enumerate(((a, oa), (b, ob), (c, oc))):
        for i in range(2):
            part = pl.ds(i * rows, rows)
            into = pltpu.make_async_copy(src.at[0, part], buf.at[o, part], isem.at[o, i])
            into.start()
            pairs.append((into, pltpu.make_async_copy(buf.at[o, part], dst.at[0, part], osem.at[o, i])))
    for into, out in pairs:
        into.wait()
        out.start()
    for _, out in pairs:
        out.wait()


def body(n_seq, n_dp, out_grad, w_out, queries, keys, values, keep_bits, query_later):
    T, D = out_grad.shape[1:]
    I = queries.shape[2]
    Wr = w_out.shape[0]
    Fc = 2 * Wr
    Hc = Fc // HD
    X = n_dp // 2
    H = I // HD
    kgn = len(split(0, H, 4))
    qgn = len(split(0, Hc, 4)) + (X - 1) * len(split(0, Hc, 1))
    state = pltpu.VMEM((H, HD, HD), BF)
    dma = pltpu.SemaphoreType.DMA
    far = max(X - 1, 1)
    scratch = [
        pltpu.VMEM((2, Wr, D), BF),
        pltpu.VMEM((T, D), BF),
        pltpu.VMEM((far, T, D), BF),
        pltpu.VMEM((T, I), BF),
        pltpu.VMEM((T, I), BF),
        pltpu.VMEM((T, I), BF),
        pltpu.VMEM((T, keep_bits.shape[2]), jnp.int32),
        pltpu.VMEM((H, HD, HD), F32),
        pltpu.VMEM((X, T, Fc), BF),
        pltpu.VMEM((T, I), BF),
        pltpu.VMEM((far, T, Fc), BF),
        state, state, state, state, state,
        state, state, state, state, state,
        pltpu.VMEM((H, T, HD), F32),
        pltpu.VMEM((H, T, HD), F32),
        pltpu.VMEM((H, T, HD), F32),
        pltpu.VMEM((3, T, I), BF),
        dma((7,)), dma((2,)),
        dma((NC, far)), dma((NC, far)), dma((2, NC, far)), dma((2, NC, far)),
        dma((kgn,)), dma((kgn,)), dma((kgn,)), dma((kgn,)),
        dma((qgn,)), dma((qgn,)), dma((qgn,)), dma((qgn,)),
        dma((3, X)),
    ]
    out = jax.ShapeDtypeStruct((1, T, I), BF)
    hbm = pl.BlockSpec(memory_space=pl.ANY)
    parts = pl.pallas_call(
        functools.partial(kernel, n_seq, n_dp),
        out_shape=(out, out, out),
        in_specs=[hbm] * 7,
        out_specs=(hbm, hbm, hbm),
        scratch_shapes=scratch,
        compiler_params=pltpu.CompilerParams(
            collective_id=0, has_side_effects=True, vmem_limit_bytes=60 * 1024 * 1024
        ),
    )(out_grad, w_out, queries, keys, values, keep_bits, query_later)
    return pl.pallas_call(
        settle,
        out_shape=(out, out, out),
        in_specs=[hbm] * 3,
        out_specs=(hbm, hbm, hbm),
        scratch_shapes=[pltpu.VMEM((3, T, I), BF), dma((3, 2)), dma((3, 2))],
    )(*parts)


def solution(mesh):
    rows = P("dp", "seq", None)
    in_specs = (rows, P("dp", None), rows, rows, rows, rows, P("dp", None, None, None))
    fn = functools.partial(body, mesh.shape["seq"], mesh.shape["dp"])
    return jax.shard_map(fn, mesh=mesh, in_specs=in_specs, out_specs=(rows, rows, rows), check_vma=False)
```
